128 devices in a mesh: grp: 2 (over core), row: 8 (over x_lo, y), col: 8 (over z, x_hi).
Axes of the slice: x: 4 (x_hi: 2, x_lo: 2; x = x_hi * 2 + x_lo), y: 4, z: 4, core: 2. Of those that a mesh axis runs over, the one named last changes fastest.
Arguments:
- conserved: float32 [5, 512, 4096], P(None, 'row', 'col'), may hold values from -1 to 5.5, as said below
- displacement: float32 [2, 512, 4096], P(None, ('row', 'col')), may hold values from -0.3 to 0.3
Outputs:
- group_fields: float32 [2, 5, 512, 4096], P('grp', None, 'row', 'col')
The draws below stay inside these ranges and needn't reach their ends.
Inputs may be any that keep to these rules, and one draw needn't show every extreme that they name: `conserved`: per cell: density and pressure (0.4 times the energy minus the kinetic energy) lie between 1 and 2, both speeds between -0.5 and 0.5, the tracer fraction between 0 and 1.
All inputs are finite; a program needn't handle non-finite values.
Results may differ from the reference program's by a relative error of at most 0.0003.
Values sent between devices are 32-bit elements; how exact they have to be, the bound alone decides.
No kernel may reach another device: no remote copies, remote signals or barrier semaphores. Data moves between devices by JAX's collectives and lax.ppermute only.
A program may use at most 64 MiB of HBM per device.

```python
import jax
import jax.numpy as jnp
from jax import lax

STEPS = 2
SWEEPS = 4
NR = 512
NC = 4096


def draw_conserved(key, part):
    subkeys = jax.random.split(key, 5)
    grid_shape = (NR, NC)
    density = jax.random.uniform(subkeys[0], grid_shape, jnp.float32, 1.0, 2.0)
    speed_x = jax.random.uniform(subkeys[1], grid_shape, jnp.float32, -0.5, 0.5)
    speed_y = jax.random.uniform(subkeys[2], grid_shape, jnp.float32, -0.5, 0.5)
    pressure = jax.random.uniform(subkeys[3], grid_shape, jnp.float32, 1.0, 2.0)
    tracer = jax.random.uniform(subkeys[4], grid_shape, jnp.float32)
    energy = pressure / 0.4 + 0.5 * density * (speed_x * speed_x + speed_y * speed_y)
    return jnp.stack([density, density * speed_x, density * speed_y, energy, density * tracer]).astype(jnp.float32)


def level_of(stream_key, shape, pieces, smallest, top_value):
    factor_of, own = 1.0, jax.random.fold_in(stream_key, 6)
    for axis_at, parts in pieces:
        steps = jnp.exp(jax.random.uniform(jax.random.fold_in(own, axis_at), (parts,), jnp.float32, smallest / len(pieces), top_value / len(pieces)))
        factor_of = factor_of * jnp.repeat(steps, shape[axis_at] // parts).reshape([-1 if axis == axis_at else 1 for axis in range(len(shape))])
    return factor_of


def setup_inputs(seed: int = 0) -> dict:
    seeds = jax.random.split(jax.random.key(seed), 3)
    return {
        "conserved": draw_conserved(jax.random.fold_in(seeds[2], 71), 0),
        "displacement": jnp.clip(jax.random.uniform(seeds[1], (2, NR, NC), jnp.float32, -0.3, 0.3) * level_of(seeds[1], (2, NR, NC), ((1, 64),), -0.4, 0.0), -0.3, 0.3),
    }


HEAT_RATIO = 1.4
TIME_STEP = 0.08
GRADIENT_GAIN = 8.0
MONITOR_GAIN = 0.2
RELAXATION = 0.5

def minmod(lower_diff, upper_diff):
    smaller = jnp.where(jnp.abs(lower_diff) < jnp.abs(upper_diff), lower_diff, upper_diff)
    return jnp.where(lower_diff * upper_diff > 0.0, smaller, 0.0)

def primitives(fields):
    density = fields[0]
    speed_x = fields[1] / density
    speed_y = fields[2] / density
    pressure = (HEAT_RATIO - 1.0) * (fields[3] - 0.5 * (fields[1] * speed_x + fields[2] * speed_y))
    tracer = fields[4] / density
    return jnp.stack([density, speed_x, speed_y, pressure, tracer])

def normal_flux(states, normal_x, normal_y):
    density, speed_x, speed_y, pressure, tracer = (states[0], states[1], states[2], states[3], states[4])
    normal_speed = speed_x * normal_x + speed_y * normal_y
    energy = pressure / (HEAT_RATIO - 1.0) + 0.5 * density * (speed_x * speed_x + speed_y * speed_y)
    conserved = jnp.stack([density, density * speed_x, density * speed_y, energy, density * tracer])
    flux_terms = jnp.stack([density * normal_speed, density * speed_x * normal_speed + pressure * normal_x, density * speed_y * normal_speed + pressure * normal_y, (energy + pressure) * normal_speed, density * tracer * normal_speed])
    wave_speed = jnp.abs(normal_speed) + jnp.sqrt(HEAT_RATIO * pressure / density) * jnp.sqrt(normal_x * normal_x + normal_y * normal_y)
    return (conserved, flux_terms, wave_speed)

def rusanov(left_state, right_state, normal_x, normal_y):
    cons_left, flux_left, wave_left = normal_flux(left_state, normal_x, normal_y)
    cons_right, flux_right, wave_right = normal_flux(right_state, normal_x, normal_y)
    wave_speed = jnp.maximum(wave_left, wave_right)
    return 0.5 * (flux_left + flux_right) - 0.5 * wave_speed * (cons_right - cons_left)

def face_states(primitive, along_axis):
    extent = primitive.shape[along_axis]
    differences = lax.slice_in_dim(primitive, 1, extent, axis=along_axis) - lax.slice_in_dim(primitive, 0, extent - 1, axis=along_axis)
    slopes = minmod(lax.slice_in_dim(differences, 0, extent - 2, axis=along_axis), lax.slice_in_dim(differences, 1, extent - 1, axis=along_axis))
    left_state = lax.slice_in_dim(primitive, 1, extent - 2, axis=along_axis) + 0.5 * lax.slice_in_dim(slopes, 0, extent - 3, axis=along_axis)
    right_state = lax.slice_in_dim(primitive, 2, extent - 1, axis=along_axis) - 0.5 * lax.slice_in_dim(slopes, 1, extent - 2, axis=along_axis)
    return (left_state, right_state)

def advance(extended):
    primitive = primitives(extended[:5])
    shift_x = extended[5]
    shift_y = extended[6]
    slope_x_col = 1.0 + 0.5 * (shift_x[1:-1, 2:] - shift_x[1:-1, :-2])
    slope_x_row = 0.5 * (shift_x[2:, 1:-1] - shift_x[:-2, 1:-1])
    slope_y_col = 0.5 * (shift_y[1:-1, 2:] - shift_y[1:-1, :-2])
    slope_y_row = 1.0 + 0.5 * (shift_y[2:, 1:-1] - shift_y[:-2, 1:-1])
    normal_x = 0.5 * (slope_y_row[1:-1, :-1] + slope_y_row[1:-1, 1:])
    normal_y = -0.5 * (slope_x_row[1:-1, :-1] + slope_x_row[1:-1, 1:])
    left_state, right_state = face_states(primitive[:, 2:-2, :], 2)
    col_flux = rusanov(left_state, right_state, normal_x, normal_y)
    normal_x = -0.5 * (slope_y_col[:-1, 1:-1] + slope_y_col[1:, 1:-1])
    normal_y = 0.5 * (slope_x_col[:-1, 1:-1] + slope_x_col[1:, 1:-1])
    left_state, right_state = face_states(primitive[:, :, 2:-2], 1)
    row_flux = rusanov(left_state, right_state, normal_x, normal_y)
    jacobian = slope_x_col[1:-1, 1:-1] * slope_y_row[1:-1, 1:-1] - slope_x_row[1:-1, 1:-1] * slope_y_col[1:-1, 1:-1]
    change = col_flux[:, :, 1:] - col_flux[:, :, :-1] + (row_flux[:, 1:, :] - row_flux[:, :-1, :])
    return extended[:5, 2:-2, 2:-2] - TIME_STEP / jacobian * change

def monitor(density, pressure):
    density_col = 0.5 * (density[1:-1, 2:] - density[1:-1, :-2])
    density_row = 0.5 * (density[2:, 1:-1] - density[:-2, 1:-1])
    pressure_col = 0.5 * (pressure[1:-1, 2:] - pressure[1:-1, :-2])
    pressure_row = 0.5 * (pressure[2:, 1:-1] - pressure[:-2, 1:-1])
    strength = GRADIENT_GAIN * (density_col * density_col + density_row * density_row + pressure_col * pressure_col + pressure_row * pressure_row)
    return 1.0 + MONITOR_GAIN * strength / (1.0 + strength)

def jacobi(shifts, weight):
    center = weight[1:-1, 1:-1]
    east_face = 0.5 * (center + weight[1:-1, 2:])
    west_face = 0.5 * (center + weight[1:-1, :-2])
    north_face = 0.5 * (center + weight[2:, 1:-1])
    south_face = 0.5 * (center + weight[:-2, 1:-1])
    face_total = east_face + west_face + north_face + south_face
    middle = shifts[:, 1:-1, 1:-1]
    beside_all = east_face * shifts[:, 1:-1, 2:] + west_face * shifts[:, 1:-1, :-2] + north_face * shifts[:, 2:, 1:-1] + south_face * shifts[:, :-2, 1:-1]
    source = jnp.stack([east_face - west_face, north_face - south_face])
    target = (beside_all + source) / face_total
    return middle + RELAXATION * (target - middle)

def wrap_fields(values, margin):
    return jnp.pad(values, ((0, 0), (margin, margin), (margin, margin)), mode='wrap')

def wrap_plane(values, margin):
    return jnp.pad(values, ((margin, margin), (margin, margin)), mode='wrap')

def reference(conserved, displacement):
    current = conserved
    shifts = displacement
    previous = shifts
    weight = jnp.zeros(shifts.shape[1:], jnp.float32)
    for step_index in range(STEPS):
        primitive = primitives(current)
        padded = wrap_fields(jnp.stack([primitive[0], primitive[3]]), 1)
        weight = monitor(padded[0], padded[1])
        start_shifts = shifts
        for sweep_index in range(SWEEPS):
            shifts = jacobi(wrap_fields(shifts, 1), wrap_plane(weight, 1))
        current = advance(wrap_fields(jnp.concatenate([current, start_shifts]), 2))
        previous = start_shifts
    mesh_fields = jnp.stack([shifts[0], shifts[1], (shifts[0] - previous[0]) / TIME_STEP, (shifts[1] - previous[1]) / TIME_STEP, weight])
    return jnp.stack([current, mesh_fields])
```

```python
import jax
import jax.numpy as jnp
from jax import lax
from jax.sharding import PartitionSpec as P

STEPS = 2
SWEEPS = 4


HEAT_RATIO = 1.4
TIME_STEP = 0.08
GRADIENT_GAIN = 8.0
MONITOR_GAIN = 0.2
RELAXATION = 0.5


def with_halo(cells, sides, width):
    for axis, dim in sides:
        count = lax.axis_size(axis)
        head = lax.slice_in_dim(cells, 0, width, axis=dim)
        tail = lax.slice_in_dim(cells, cells.shape[dim] - width, cells.shape[dim], axis=dim)
        cells = jnp.concatenate(
            [
                lax.ppermute(tail, axis, [(i, (i + 1) % count) for i in range(count)]),
                cells,
                lax.ppermute(head, axis, [((i + 1) % count, i) for i in range(count)]),
            ],
            axis=dim,
        )
    return cells


def minmod(lower_diff, upper_diff):
    smaller = jnp.where(jnp.abs(lower_diff) < jnp.abs(upper_diff), lower_diff, upper_diff)
    return jnp.where(lower_diff * upper_diff > 0.0, smaller, 0.0)


def primitives(fields):
    density = fields[0]
    speed_x = fields[1] / density
    speed_y = fields[2] / density
    pressure = (HEAT_RATIO - 1.0) * (fields[3] - 0.5 * (fields[1] * speed_x + fields[2] * speed_y))
    tracer = fields[4] / density
    return jnp.stack([density, speed_x, speed_y, pressure, tracer])


def normal_flux(states, normal_x, normal_y):
    density, speed_x, speed_y, pressure, tracer = (
        states[0],
        states[1],
        states[2],
        states[3],
        states[4],
    )
    normal_speed = speed_x * normal_x + speed_y * normal_y
    energy = pressure / (HEAT_RATIO - 1.0) + 0.5 * density * (speed_x * speed_x + speed_y * speed_y)
    conserved = jnp.stack([density, density * speed_x, density * speed_y, energy, density * tracer])
    flux_terms = jnp.stack(
        [
            density * normal_speed,
            density * speed_x * normal_speed + pressure * normal_x,
            density * speed_y * normal_speed + pressure * normal_y,
            (energy + pressure) * normal_speed,
            density * tracer * normal_speed,
        ]
    )
    wave_speed = jnp.abs(normal_speed) + jnp.sqrt(HEAT_RATIO * pressure / density) * jnp.sqrt(
        normal_x * normal_x + normal_y * normal_y
    )
    return (conserved, flux_terms, wave_speed)


def rusanov(left_state, right_state, normal_x, normal_y):
    cons_left, flux_left, wave_left = normal_flux(left_state, normal_x, normal_y)
    cons_right, flux_right, wave_right = normal_flux(right_state, normal_x, normal_y)
    wave_speed = jnp.maximum(wave_left, wave_right)
    return 0.5 * (flux_left + flux_right) - 0.5 * wave_speed * (cons_right - cons_left)


def face_states(primitive, along_axis):
    extent = primitive.shape[along_axis]
    differences = lax.slice_in_dim(primitive, 1, extent, axis=along_axis) - lax.slice_in_dim(
        primitive, 0, extent - 1, axis=along_axis
    )
    slopes = minmod(
        lax.slice_in_dim(differences, 0, extent - 2, axis=along_axis),
        lax.slice_in_dim(differences, 1, extent - 1, axis=along_axis),
    )
    left_state = lax.slice_in_dim(
        primitive, 1, extent - 2, axis=along_axis
    ) + 0.5 * lax.slice_in_dim(slopes, 0, extent - 3, axis=along_axis)
    right_state = lax.slice_in_dim(
        primitive, 2, extent - 1, axis=along_axis
    ) - 0.5 * lax.slice_in_dim(slopes, 1, extent - 2, axis=along_axis)
    return (left_state, right_state)


def advance(extended):
    primitive = primitives(extended[:5])
    shift_x = extended[5]
    shift_y = extended[6]
    slope_x_col = 1.0 + 0.5 * (shift_x[1:-1, 2:] - shift_x[1:-1, :-2])
    slope_x_row = 0.5 * (shift_x[2:, 1:-1] - shift_x[:-2, 1:-1])
    slope_y_col = 0.5 * (shift_y[1:-1, 2:] - shift_y[1:-1, :-2])
    slope_y_row = 1.0 + 0.5 * (shift_y[2:, 1:-1] - shift_y[:-2, 1:-1])
    normal_x = 0.5 * (slope_y_row[1:-1, :-1] + slope_y_row[1:-1, 1:])
    normal_y = -0.5 * (slope_x_row[1:-1, :-1] + slope_x_row[1:-1, 1:])
    left_state, right_state = face_states(primitive[:, 2:-2, :], 2)
    col_flux = rusanov(left_state, right_state, normal_x, normal_y)
    normal_x = -0.5 * (slope_y_col[:-1, 1:-1] + slope_y_col[1:, 1:-1])
    normal_y = 0.5 * (slope_x_col[:-1, 1:-1] + slope_x_col[1:, 1:-1])
    left_state, right_state = face_states(primitive[:, :, 2:-2], 1)
    row_flux = rusanov(left_state, right_state, normal_x, normal_y)
    jacobian = (
        slope_x_col[1:-1, 1:-1] * slope_y_row[1:-1, 1:-1]
        - slope_x_row[1:-1, 1:-1] * slope_y_col[1:-1, 1:-1]
    )
    change = col_flux[:, :, 1:] - col_flux[:, :, :-1] + (row_flux[:, 1:, :] - row_flux[:, :-1, :])
    return extended[:5, 2:-2, 2:-2] - TIME_STEP / jacobian * change


def monitor(density, pressure):
    density_col = 0.5 * (density[1:-1, 2:] - density[1:-1, :-2])
    density_row = 0.5 * (density[2:, 1:-1] - density[:-2, 1:-1])
    pressure_col = 0.5 * (pressure[1:-1, 2:] - pressure[1:-1, :-2])
    pressure_row = 0.5 * (pressure[2:, 1:-1] - pressure[:-2, 1:-1])
    strength = GRADIENT_GAIN * (
        density_col * density_col
        + density_row * density_row
        + pressure_col * pressure_col
        + pressure_row * pressure_row
    )
    return 1.0 + MONITOR_GAIN * strength / (1.0 + strength)


def jacobi(shifts, weight):
    center = weight[1:-1, 1:-1]
    east_face = 0.5 * (center + weight[1:-1, 2:])
    west_face = 0.5 * (center + weight[1:-1, :-2])
    north_face = 0.5 * (center + weight[2:, 1:-1])
    south_face = 0.5 * (center + weight[:-2, 1:-1])
    face_total = east_face + west_face + north_face + south_face
    middle = shifts[:, 1:-1, 1:-1]
    beside_all = (
        east_face * shifts[:, 1:-1, 2:]
        + west_face * shifts[:, 1:-1, :-2]
        + north_face * shifts[:, 2:, 1:-1]
        + south_face * shifts[:, :-2, 1:-1]
    )
    source = jnp.stack([east_face - west_face, north_face - south_face])
    target = (beside_all + source) / face_total
    return middle + RELAXATION * (target - middle)


HALO = 9


def crop(values, width):
    return values[..., width:-width, width:-width]


def relax(shifts, weight):
    for sweep_index in range(SWEEPS):
        shifts = jacobi(shifts, weight)
        weight = crop(weight, 1)
    return shifts


def monitor_of(fields):
    primitive = primitives(fields)
    return monitor(primitive[0], primitive[3])


def gas_step(extended):
    first = relax(crop(extended[5:], 3), monitor_of(crop(extended[:5], 2)))
    state = advance(crop(extended, 5))
    return advance(jnp.concatenate([state, first]))


def mesh_step(extended):
    first = relax(crop(extended[5:], 1), monitor_of(extended[:5]))
    state = advance(crop(extended, 2))
    weight = monitor_of(state)
    second = relax(first, weight)
    velocity = (second - crop(first, 4)) / TIME_STEP
    return jnp.concatenate([second, velocity, crop(weight, 4)[None]])


def on_device(conserved, displacement):
    on_mesh = lax.axis_index("grp") == 1
    column_count = lax.axis_size("col")
    block_rows = conserved.shape[1]
    block_cols = conserved.shape[2]
    wide = jnp.concatenate(
        [displacement[:, :, -HALO:], displacement, displacement[:, :, :HALO]], axis=2
    )
    pieces = jnp.stack(
        [
            wide[:, :, c * block_cols : (c + 1) * block_cols + 2 * HALO]
            for c in range(column_count)
        ],
        axis=1,
    )
    arrived = lax.all_to_all(pieces, "col", split_axis=1, concat_axis=1, tiled=True)
    shifts = arrived.reshape(2, block_rows, block_cols + 2 * HALO)
    fields = with_halo(conserved, (("col", 2),), HALO)
    extended = with_halo(jnp.concatenate([fields, shifts]), (("row", 1),), HALO)
    return lax.cond(on_mesh, mesh_step, gas_step, extended)[None]


def solution(mesh):
    placed = (P(None, "row", "col"), P(None, ("row", "col"), None))
    return jax.shard_map(
        on_device,
        mesh=mesh,
        in_specs=placed,
        out_specs=P("grp", None, "row", "col"),
        check_vma=False,
    )
```
